256 devices in a mesh: ctx: 64 (over z, x, core), rows: 4 (over y).
Axes of the slice: x: 4, y: 4, z: 8, core: 2. Of those that a mesh axis runs over, the one named last changes fastest.
Arguments:
- hidden: bfloat16 [2, 4, 8192], P(None, 'rows'), may hold values from -6 to 6
- norm_gain: bfloat16 [8192], replicated, may hold values from 0.099609375 to 1.8984375
- w_query: bfloat16 [8192, 8192], P(None, 'ctx'), may hold values from -2 to 2
- w_key: bfloat16 [8192, 1024], P(None, 'ctx'), may hold values from -2 to 2
- w_value: bfloat16 [8192, 1024], P(None, 'ctx'), may hold values from -0.0625 to 0.0625
- w_out: bfloat16 [8192, 8192], P('ctx'), may hold values from -0.0625 to 0.0625
- cache_keys: bfloat16 [4, 131072, 8, 128], P('rows', 'ctx'), may hold values from -1200 to 1200
- cache_values: bfloat16 [4, 131072, 8, 128], P('rows', 'ctx'), may hold values from -24 to 24
- lengths: int32 [4], P('rows'), may hold values from 1 to 131072, as said below
- positions: int32 [4], P('rows'), may hold values from 0 to 8191
Outputs:
- attended: bfloat16 [2, 8192, 4], P(None, 'ctx', 'rows')
The draws below stay inside these ranges and needn't reach their ends.
Inputs may be any that keep to these rules, and one draw needn't show every extreme that they name: `lengths`: one sequence has exactly 131072 live tokens and another at most 32; slots at or past a sequence's length hold entries that must not be read.
All inputs are finite; a program needn't handle non-finite values.
Results may differ from the reference program's by a relative error of at most 0.02.
The reference program's roundings to bfloat16 on the way count: a program that leaves them out, or rounds other values in their place, can miss the bound.
Values may be sent and summed in bfloat16 or wider, within the bound.
A program may use at most 64 MiB of HBM per device.

```python
import math
import jax
import jax.numpy as jnp
from jax import lax

D = 8192
H = 64
KV = 8
HD = 128
STEPS = 2
CACHE = 131072
ROWS = 4


def projection_pair(key):
    group = H // KV
    spread = 1.0 / math.sqrt(D)
    query_part = jax.random.truncated_normal(jax.random.fold_in(key, 31), -4.0, 4.0, (D, H * HD), jnp.float32) * spread
    noise_part = jax.random.truncated_normal(jax.random.fold_in(key, 37), -4.0, 4.0, (D, KV * HD), jnp.float32)
    matched = query_part.reshape(D, KV, group, HD)[:, :, 0, :].reshape(D, KV * HD)
    key_part = 1.8 * matched + 0.5 * spread * noise_part
    return (query_part, key_part)


def draw_w_query(key, part):
    return projection_pair(key)[0].astype(jnp.bfloat16)


def draw_w_key(key, part):
    return projection_pair(key)[1].astype(jnp.bfloat16)


def draw_cache_keys(key, part):
    shape = (ROWS, CACHE, KV, HD)
    base = jax.random.normal(key, shape, jnp.float32) * 3.0
    return base.astype(jnp.bfloat16)


def draw_lengths(key, part):
    topmost = CACHE.bit_length() - 1
    spread = jax.random.randint(jax.random.fold_in(key, 1), (ROWS,), 4, topmost + 1)
    capped = jnp.left_shift(jnp.ones((ROWS,), jnp.int32), spread)
    drawn = jax.random.randint(jax.random.fold_in(key, 2), (ROWS,), 1, capped + 1)
    full_row = jax.random.randint(jax.random.fold_in(key, 3), (), 0, ROWS)
    short_row = (full_row + jax.random.randint(jax.random.fold_in(key, 4), (), 1, ROWS)) % ROWS
    short_len = jax.random.randint(jax.random.fold_in(key, 5), (), 1, 33)
    row_ids = jnp.arange(ROWS)
    drawn = jnp.where(row_ids == short_row, short_len, drawn)
    return jnp.where(row_ids == full_row, CACHE, drawn).astype(jnp.int32)


def touch_ends(values, key, least, top_value):
    longest = values.shape.index(max(values.shape))
    spots = []
    for shift in (0, 1):
        where = [jax.random.randint(jax.random.fold_in(key, axis), (), 0, length) for axis, length in enumerate(values.shape)]
        where[longest] = (where[longest] + shift) % values.shape[longest]
        spots.append(tuple(where))
    return values.at[spots[0]].set(least).at[spots[1]].set(top_value)


def block_scale(key, dims, split, low, top_value):
    factor_of, own = 1.0, jax.random.fold_in(key, 6)
    for axis_at, shards_of in split:
        heights = jnp.exp(jax.random.uniform(jax.random.fold_in(own, axis_at), (shards_of,), jnp.float32, low / len(split), top_value / len(split)))
        factor_of = factor_of * jnp.repeat(heights, dims[axis_at] // shards_of).reshape([-1 if axis == axis_at else 1 for axis in range(len(dims))])
    return factor_of


def bell_draw(own_key, shape, deviation, reach, shards=(), kind=jnp.bfloat16):
    result = jax.random.normal(own_key, shape, jnp.float32) * deviation
    if len(shards) > 0:
        result = block_scale(own_key, shape, shards, -0.22, 0.18) * result
    return jnp.clip(result, min=-reach, max=reach).astype(kind)


def setup_inputs(seed: int = 0) -> dict:
    key_of = jax.random.split(jax.random.key(seed), 11)
    hidden = bell_draw(key_of[0], (STEPS, ROWS, D), 1.0, 6.0, ((1, 4),))
    norm_gain = jnp.clip(1.0 + 0.18 * jax.random.normal(key_of[1], (D,), jnp.float32), 0.099609375, 1.8984375).astype(jnp.bfloat16)
    w_query = draw_w_query(jax.random.fold_in(key_of[10], 71), 0)
    w_key = draw_w_key(jax.random.fold_in(key_of[10], 71), 0)
    w_value = bell_draw(key_of[4], (D, KV * HD), D ** -0.5, 0.0625, ((1, 64),))
    w_out = bell_draw(key_of[5], (H * HD, D), (H * HD) ** -0.5, 0.0625, ((0, 64),))
    cache_keys = draw_cache_keys(jax.random.fold_in(key_of[10], 71), 0)
    cache_values = bell_draw(key_of[7], (ROWS, CACHE, KV, HD), 4.0, 24.0, ((0, 4), (1, 64)))
    lengths = draw_lengths(jax.random.fold_in(key_of[10], 71), 0)
    positions = touch_ends(jax.random.randint(key_of[9], (ROWS,), 0, 8192), jax.random.fold_in(key_of[9], 1), 0, 8191).astype(jnp.int32)
    return {"hidden": hidden, "norm_gain": norm_gain, "w_query": w_query, "w_key": w_key, "w_value": w_value, "w_out": w_out, "cache_keys": cache_keys, "cache_values": cache_values, "lengths": lengths, "positions": positions}


theta_base = 500000.0
epsilon = 1e-05

def rotate(vectors, places):
    halfway = vectors.shape[-1] // 2
    inverse = theta_base ** (-(jnp.arange(halfway, dtype=jnp.float32) * 2.0 / vectors.shape[-1]))
    angles = places.astype(jnp.float32)[:, None, None] * inverse
    cosines = jnp.cos(angles)
    sines = jnp.sin(angles)
    leading = vectors[..., :halfway]
    trailing = vectors[..., halfway:]
    return jnp.concatenate([leading * cosines - trailing * sines, trailing * cosines + leading * sines], -1)

def normalize(inputs, norm_gain):
    floats = inputs.astype(jnp.float32)
    scaled = floats * lax.rsqrt(lax.optimization_barrier(jnp.mean(floats * floats, -1, keepdims=True)) + epsilon)
    return (scaled * norm_gain.astype(jnp.float32)).astype(jnp.bfloat16)

def attend_row(operands):
    queries, keys_row, values_row, length, own_keys, own_values = operands
    head_size = keys_row.shape[2]
    scale_factor = 1.0 / math.sqrt(head_size)
    visible = (jnp.arange(keys_row.shape[0]) < length)[None, :]

    def per_group(kv_index):
        group_query = queries[kv_index]
        group_keys = lax.dynamic_index_in_dim(keys_row, kv_index, 1, keepdims=False)
        group_values = lax.dynamic_index_in_dim(values_row, kv_index, 1, keepdims=False)
        fresh_keys = lax.dynamic_index_in_dim(own_keys, kv_index, 1, keepdims=False)
        fresh_values = lax.dynamic_index_in_dim(own_values, kv_index, 1, keepdims=False)
        cached = jnp.dot(group_query, group_keys.T, preferred_element_type=jnp.float32) * scale_factor
        cached = jnp.where(visible, cached, -1e+30)
        fresh = jnp.dot(group_query, fresh_keys.T, preferred_element_type=jnp.float32) * scale_factor
        highest = jnp.maximum(lax.optimization_barrier(jnp.max(cached, -1)), lax.optimization_barrier(jnp.max(fresh, -1)))
        weights = jnp.where(visible, jnp.exp(cached - highest[:, None]), 0.0)
        fresh_weights = jnp.exp(fresh - highest[:, None])
        totals = lax.optimization_barrier(jnp.sum(weights, -1)) + lax.optimization_barrier(jnp.sum(fresh_weights, -1))
        numer = jnp.dot(weights.astype(jnp.bfloat16), group_values, preferred_element_type=jnp.float32)
        numer = numer + jnp.dot(fresh_weights.astype(jnp.bfloat16), fresh_values, preferred_element_type=jnp.float32)
        return (numer / totals[:, None]).astype(jnp.bfloat16)
    return lax.map(per_group, jnp.arange(keys_row.shape[1], dtype=jnp.int32))

def reference(hidden, norm_gain, w_query, w_key, w_value, w_out, cache_keys, cache_values, lengths, positions):
    head_size = cache_keys.shape[3]
    kv_heads = cache_keys.shape[2]
    total_heads = w_query.shape[1] // head_size
    group_size = total_heads // kv_heads
    row_count = hidden.shape[1]
    fresh_keys = []
    fresh_values = []
    results = []
    for step_index in range(hidden.shape[0]):
        layer_in = hidden[step_index].astype(jnp.float32)
        normed = normalize(layer_in, norm_gain)
        raw_query = jnp.dot(normed, w_query, preferred_element_type=jnp.float32).astype(jnp.bfloat16)
        raw_key = jnp.dot(normed, w_key, preferred_element_type=jnp.float32).astype(jnp.bfloat16)
        raw_value = jnp.dot(normed, w_value, preferred_element_type=jnp.float32).astype(jnp.bfloat16)
        places = positions + step_index
        queries = rotate(raw_query.astype(jnp.float32).reshape(row_count, total_heads, head_size), places).astype(jnp.bfloat16)
        new_keys = rotate(raw_key.astype(jnp.float32).reshape(row_count, kv_heads, head_size), places).astype(jnp.bfloat16)
        fresh_keys.append(new_keys)
        fresh_values.append(raw_value.reshape(row_count, kv_heads, head_size))
        grouped = queries.reshape(row_count, kv_heads, group_size, head_size)
        heads_out = lax.map(attend_row, (grouped, cache_keys, cache_values, lengths, jnp.stack(fresh_keys, 1), jnp.stack(fresh_values, 1)))
        flat = heads_out.reshape(row_count, total_heads * head_size)
        attended = jnp.dot(flat, w_out, preferred_element_type=jnp.float32).astype(jnp.bfloat16)
        results.append(attended.T)
    return jnp.stack(results, 0)
```

```python
import functools
import math

import jax
import jax.numpy as jnp
import numpy as np
from jax import lax
from jax.experimental import pallas as pl
from jax.experimental.pallas import tpu as pltpu
from jax.sharding import PartitionSpec as P

theta_base = 500000.0
epsilon = 1e-05
NEG = -1e30
LANES = 128
MESH = pl.DeviceIdType.MESH
F32 = jnp.float32
BF16 = jnp.bfloat16


def to(peer):
    return {"ctx": peer}


def lane_class_reduce(x, op, period):
    shift = period
    while shift < LANES:
        x = op(x, pltpu.roll(x, shift, 1))
        shift *= 2
    return x


def kernel(
    dims,
    pos_hbm, len_hbm, hid_hbm, gain_hbm, inv_hbm, wq_hbm, wk_hbm, wv_hbm, wo_hbm, kc_hbm, vc_hbm,
    out_ref,
    pos_s, len_s, hid, gain, inv, wq, wk, wv, wo, kc, vc,
    q_in, kv_out, kv_in, scores, part_out, part_in, proj_out, proj_in,
    load_sem, send_sem, recv_sem,
):
    n, group, steps, chunks, scale = dims
    me = lax.axis_index("ctx")
    plane = me // group
    seat = me % group
    rows = 2 * group
    total = kc.shape[0]
    width = total // chunks

    loads = {}
    pairs = (
        (hid_hbm, hid), (gain_hbm, gain), (pos_hbm, pos_s), (len_hbm, len_s), (inv_hbm, inv),
        (wq_hbm, wq), (wk_hbm, wk), (wv_hbm, wv), (kc_hbm, kc), (vc_hbm, vc), (wo_hbm, wo),
    )
    names = ("hid", "gain", "pos", "len", "inv", "wq", "wk", "wv", "kc", "vc", "wo")
    for i, (name, (src, dst)) in enumerate(zip(names, pairs)):
        loads[name] = pltpu.make_async_copy(src, dst, load_sem.at[i])
        loads[name].start()

    barrier = pltpu.get_barrier_semaphore()

    def greet(p, carry):
        pl.semaphore_signal(barrier, inc=1, device_id=to((me + p) % n), device_id_type=MESH)
        return carry

    lax.fori_loop(1, n, greet, 0)

    loads["hid"].wait()
    loads["gain"].wait()
    x = hid[...].astype(F32)
    x = x * lax.rsqrt(jnp.mean(x * x, -1, keepdims=True) + epsilon)
    normed = jnp.concatenate(
        [
            (x[:, LANES * r : LANES * (r + 1)] * gain[r : r + 1, :].astype(F32)).astype(BF16)
            for r in range(gain.shape[0])
        ],
        axis=1,
    )
    loads["pos"].wait()
    loads["inv"].wait()
    step_row = lax.broadcasted_iota(jnp.int32, (steps, LANES), 0)
    lane2 = lax.broadcasted_iota(jnp.int32, (steps, LANES), 1)
    angles = (pos_s[0] + step_row).astype(F32) * inv[0:1, :]
    cosines = jnp.cos(angles)
    sines = jnp.where(lane2 < LANES // 2, -1.0, 1.0) * jnp.sin(angles)

    def rotary(u):
        return (u * cosines + pltpu.roll(u, LANES // 2, 1) * sines).astype(BF16)

    nt = (((1,), (1,)), ((), ()))
    loads["wk"].wait()
    loads["wv"].wait()
    kv_out[...] = jnp.zeros(kv_out.shape, BF16)
    wide = wk.shape[0]
    kv_out[0:2, 0:wide] = lax.dot_general(normed, wk[...], nt, preferred_element_type=F32).astype(BF16)
    kv_out[2:4, 0:wide] = lax.dot_general(normed, wv[...], nt, preferred_element_type=F32).astype(BF16)
    loads["wq"].wait()
    raw = jnp.dot(normed, wq[...], preferred_element_type=F32).astype(BF16).astype(F32)
    q_own = rotary(raw)
    q_in[me] = q_own
    kv_in[seat] = kv_out[...]

    pl.semaphore_wait(barrier, n - 1)

    def send_q(p, carry):
        pltpu.make_async_remote_copy(
            q_in.at[me], q_in.at[me], send_sem.at[0], recv_sem.at[0],
            device_id=to((me + p) % n), device_id_type=MESH,
        ).start()
        return carry

    lax.fori_loop(1, n, send_q, 0)

    def send_kv(p, carry):
        pltpu.make_async_remote_copy(
            kv_out, kv_in.at[seat], send_sem.at[1], recv_sem.at[1],
            device_id=to(plane * group + (seat + p) % group), device_id_type=MESH,
        ).start()
        return carry

    lax.fori_loop(1, group, send_kv, 0)

    def wait_all(buf, count, k):
        views = buf.at[pl.ds(0, count)]
        both = pltpu.make_async_remote_copy(
            views, views, send_sem.at[k], recv_sem.at[k],
            device_id=to((me + 1) % n), device_id_type=MESH,
        )
        both.wait_recv()
        both.wait_send()

    loads["kc"].wait()
    loads["len"].wait()
    wait_all(q_in, n - 1, 0)

    live = jnp.clip(len_s[0] - me * (total // group), 0, total // group) * group
    lane_w = lax.broadcasted_iota(jnp.int32, (rows, width), 1)
    head_w = lane_w % group
    queries = q_in[...].reshape(n * steps, LANES)

    def score(c, top):
        keys = kc[pl.ds(pl.multiple_of(c * width, width), width), :]
        every = lax.dot_general(queries, keys, nt, preferred_element_type=F32)
        mine = every[0:rows]
        for g in range(1, n // group):
            mine = jnp.where(head_w == g, every[rows * g : rows * (g + 1)], mine)
        mine = jnp.where(lane_w + c * width < live, mine * scale, NEG)
        scores[c] = mine
        for t in range(width // LANES):
            top = jnp.maximum(top, mine[:, LANES * t : LANES * (t + 1)])
        return top

    top = lax.fori_loop(0, chunks, score, jnp.full((rows, LANES), NEG, F32))
    top = lane_class_reduce(top, jnp.maximum, group)

    loads["vc"].wait()
    lane_r = lax.broadcasted_iota(jnp.int32, (rows, LANES), 1)
    picks = [jnp.where(lane_r % group == g, 1.0, 0.0).astype(BF16) for g in range(n // group)]

    def weigh(c, carried):
        den, num = carried
        tiles = []
        for t in range(width // LANES):
            s = scores[c, :, LANES * t : LANES * (t + 1)]
            w = jnp.where(lane_r + (c * width + LANES * t) < live, jnp.exp(s - top), 0.0)
            den = den + w
            tiles.append(w.astype(BF16))
        spread = jnp.concatenate(
            [jnp.concatenate([w * pick for w in tiles], axis=1) for pick in picks], axis=0
        )
        values = vc[pl.ds(pl.multiple_of(c * width, width), width), :]
        return den, num + jnp.dot(spread, values, preferred_element_type=F32)

    den, num = lax.fori_loop(
        0, chunks, weigh,
        (jnp.zeros((rows, LANES), F32), jnp.zeros((n * steps, LANES), F32)),
    )
    den = lane_class_reduce(den, jnp.add, group)

    def terms(v, count):
        out = []
        for _ in range(count):
            head = v.astype(BF16).astype(F32)
            out.append(head)
            v = v - head
        return out

    side = jnp.zeros((rows, LANES), F32)
    for k, term in enumerate(terms(top, 3) + terms(den, 3)):
        side = jnp.where(lane_r // group == k, term, side)
    side = side.astype(BF16)
    num = num.astype(BF16)
    for h in range(n):
        j = h % group
        part_out[h, 0:2, :] = num[2 * h : 2 * h + 2]
        part_out[h, 2:4, :] = side[2 * j : 2 * j + 2]
    part_in[me] = part_out[me]

    def send_part(p, carry):
        peer = (me + p) % n
        pltpu.make_async_remote_copy(
            part_out.at[peer], part_in.at[me], send_sem.at[2], recv_sem.at[2],
            device_id=to(peer), device_id_type=MESH,
        ).start()
        return carry

    lax.fori_loop(1, n, send_part, 0)

    wait_all(kv_in, group - 1, 1)
    fresh = jnp.zeros((4, LANES), F32)
    for j in range(group):
        piece = kv_in[j].astype(F32)
        fresh = fresh + (pltpu.roll(piece, wide * j, 1) if j else piece)
    new_key = rotary(fresh[0:2]).astype(F32)
    new_val = fresh[2:4]
    qf = q_own.astype(F32)
    second = lax.broadcasted_iota(jnp.int32, (steps, 1), 0) > 0
    s0 = jnp.sum(qf * new_key[0:1], -1, keepdims=True) * scale
    s1 = jnp.sum(qf * new_key[1:2], -1, keepdims=True) * scale
    s1 = jnp.where(second, s1, NEG)

    wait_all(part_in, n - 1, 2)
    parts = part_in[...].astype(F32)
    lane_p = lax.broadcasted_iota(jnp.int32, (n, 2, LANES), 2)
    ours = lane_p % group == plane
    numer = parts[:, 0:2, :]
    extra = parts[:, 2:4, :]
    tops = jnp.sum(jnp.where(ours & (lane_p < 3 * group), extra, 0.0), -1, keepdims=True)
    dens = jnp.sum(
        jnp.where(ours & (lane_p >= 3 * group) & (lane_p < 6 * group), extra, 0.0), -1, keepdims=True
    )
    final = jnp.maximum(jnp.max(tops, 0), jnp.maximum(s0, s1))
    factor = jnp.exp(tops - final[None])
    w0 = jnp.exp(s0 - final)
    w1 = jnp.where(second, jnp.exp(s1 - final), 0.0)
    bottom = jnp.sum(factor * dens, 0) + w0 + w1
    upper = (
        jnp.sum(factor * numer, 0)
        + w0.astype(BF16).astype(F32) * new_val[0:1]
        + w1.astype(BF16).astype(F32) * new_val[1:2]
    )
    head_out = (upper / bottom).astype(BF16)

    loads["wo"].wait()
    span = group * LANES
    for k in range(1, n // group + 1):
        owner_plane = (plane + k) % (n // group)
        cols = pl.ds(pl.multiple_of(owner_plane * span, span), span)
        block = jnp.dot(head_out, wo[:, cols], preferred_element_type=F32).astype(BF16)
        for j in range(group):
            proj_out[owner_plane * group + j] = block[:, LANES * j : LANES * (j + 1)]

        def send_proj(j, carry, owner_plane=owner_plane):
            peer = owner_plane * group + (seat + j) % group
            pltpu.make_async_remote_copy(
                proj_out.at[peer], proj_in.at[me], send_sem.at[3], recv_sem.at[3],
                device_id=to(peer), device_id_type=MESH,
            ).start()
            return carry

        lax.fori_loop(1 if k == n // group else 0, group, send_proj, 0)
    proj_in[me] = proj_out[me]
    wait_all(proj_in, n - 1, 3)
    out_ref[...] = jnp.sum(proj_in[...].astype(F32), 0).astype(BF16)


def on_device(
    hidden, norm_gain, w_query, w_key, w_value, w_out, cache_keys, cache_values, lengths, positions
):
    n = lax.axis_size("ctx")
    steps, _, depth = hidden.shape
    _, span, group_count, head_size = cache_keys.shape
    group = n // group_count
    total = span * group_count
    chunks = 8
    half = head_size // 2
    inverse = theta_base ** (-(np.arange(half, dtype=np.float64) * 2.0 / head_size))
    inverse = np.tile(np.concatenate([inverse, inverse]).astype(np.float32)[None], (8, 1))
    dims = (n, group, steps, chunks, 1.0 / math.sqrt(head_size))
    anywhere = pl.BlockSpec(memory_space=pl.ANY)
    rows = 2 * group
    out = pl.pallas_call(
        functools.partial(kernel, dims),
        out_shape=jax.ShapeDtypeStruct((steps, w_out.shape[1] // n), BF16),
        in_specs=[anywhere] * 11,
        out_specs=pl.BlockSpec(memory_space=pltpu.VMEM),
        scratch_shapes=[
            pltpu.SMEM((1,), jnp.int32),
            pltpu.SMEM((1,), jnp.int32),
            pltpu.VMEM((steps, depth), BF16),
            pltpu.VMEM((depth // LANES, LANES), BF16),
            pltpu.VMEM((8, LANES), F32),
            pltpu.VMEM((depth, LANES), BF16),
            pltpu.VMEM((w_key.shape[1], depth), BF16),
            pltpu.VMEM((w_value.shape[1], depth), BF16),
            pltpu.VMEM(w_out.shape, BF16),
            pltpu.VMEM((total, head_size), BF16),
            pltpu.VMEM((total, head_size), BF16),
            pltpu.VMEM((n, steps, LANES), BF16),
            pltpu.VMEM((4, LANES), BF16),
            pltpu.VMEM((group, 4, LANES), BF16),
            pltpu.VMEM((chunks, rows, total // chunks), F32),
            pltpu.VMEM((n, 4, LANES), BF16),
            pltpu.VMEM((n, 4, LANES), BF16),
            pltpu.VMEM((n, steps, LANES), BF16),
            pltpu.VMEM((n, steps, LANES), BF16),
            pltpu.SemaphoreType.DMA((11,)),
            pltpu.SemaphoreType.DMA((4,)),
            pltpu.SemaphoreType.DMA((4,)),
        ],
        compiler_params=pltpu.CompilerParams(
            collective_id=0, has_side_effects=True, vmem_limit_bytes=48 * 1024 * 1024
        ),
        cost_estimate=pl.CostEstimate(flops=2**30, bytes_accessed=13 * 2**20, transcendentals=2**18),
        name="decode",
    )(
        positions,
        lengths,
        hidden.reshape(steps, depth),
        norm_gain.reshape(depth // LANES, LANES),
        jnp.asarray(inverse),
        w_query,
        w_key.T,
        w_value.T,
        w_out,
        cache_keys.reshape(total, head_size),
        cache_values.reshape(total, head_size),
    )
    return out[:, :, None]


def solution(mesh):
    in_specs = (
        P(None, "rows", None),
        P(),
        P(None, "ctx"),
        P(None, "ctx"),
        P(None, "ctx"),
        P("ctx", None),
        P("rows", "ctx", None, None),
        P("rows", "ctx", None, None),
        P("rows"),
        P("rows"),
    )
    out_specs = P(None, "ctx", "rows")
    return jax.shard_map(
        on_device, mesh=mesh, in_specs=in_specs, out_specs=out_specs, check_vma=False
    )
```

```python
import functools
import math

import jax
import jax.numpy as jnp
import numpy as np
from jax import lax
from jax.experimental import pallas as pl
from jax.experimental.pallas import tpu as pltpu
from jax.sharding import PartitionSpec as P

theta_base = 500000.0
epsilon = 1e-05
NEG = -1e30
LANES = 128
MESH = pl.DeviceIdType.MESH
F32 = jnp.float32
BF16 = jnp.bfloat16


def to(peer):
    return {"ctx": peer}


def lane_class_reduce(x, op, period):
    shift = period
    while shift < LANES:
        x = op(x, pltpu.roll(x, shift, 1))
        shift *= 2
    return x


def kernel(
    dims,
    pos_hbm, len_hbm, hid_hbm, gain_hbm, inv_hbm, wq_hbm, wk_hbm, wv_hbm, wo_hbm, kc_hbm, vc_hbm,
    out_ref,
    pos_s, len_s, hid, gain, inv, wq, wk, wv, wo, kc, vc,
    q_in, kv_out, kv_in, scores, part_out, part_in, proj_out, proj_in,
    load_sem, send_sem, recv_sem,
):
    n, group, steps, chunks, scale = dims
    me = lax.axis_index("ctx")
    plane = me // group
    seat = me - plane * group
    planes = n // group
    half = n // 2

    def each_peer(start, act):
        for lower in start:
            def one(i, carry, lower=lower):
                peer = lax.rem(me + i, half) + lower

                @pl.when(peer != me)
                def _():
                    act(peer)

                return carry

            lax.fori_loop(0, half, one, 0)
    rows = 2 * group
    total = kc.shape[0]
    width = total // chunks

    loads = {}

    def load(**pairs):
        for name, (src, dst) in pairs.items():
            loads[name] = pltpu.make_async_copy(src, dst, load_sem.at[len(loads)])
            loads[name].start()

    load(hid=(hid_hbm, hid), gain=(gain_hbm, gain), wq=(wq_hbm, wq), wk=(wk_hbm, wk), wv=(wv_hbm, wv))
    barrier = pltpu.get_barrier_semaphore()

    def greet(p, carry):
        pl.semaphore_signal(barrier, inc=1, device_id=to(lax.rem(me + p, n)), device_id_type=MESH)
        return carry

    lax.fori_loop(1, n, greet, 0)

    load(pos=(pos_hbm, pos_s), inv=(inv_hbm, inv), len=(len_hbm, len_s))
    load(kc=(kc_hbm, kc), vc=(vc_hbm, vc), wo=(wo_hbm, wo))

    loads["hid"].wait()
    loads["gain"].wait()
    x = hid[...].astype(F32)
    x = x * lax.rsqrt(jnp.mean(x * x, -1, keepdims=True) + epsilon)
    normed = jnp.concatenate(
        [
            (x[:, LANES * r : LANES * (r + 1)] * gain[r : r + 1, :].astype(F32)).astype(BF16)
            for r in range(gain.shape[0])
        ],
        axis=1,
    )
    loads["pos"].wait()
    loads["inv"].wait()
    step_row = lax.broadcasted_iota(jnp.int32, (steps, LANES), 0)
    lane2 = lax.broadcasted_iota(jnp.int32, (steps, LANES), 1)
    angles = (pos_s[0] + step_row).astype(F32) * inv[0:1, :]
    cosines = jnp.cos(angles)
    sines = jnp.where(lane2 < LANES // 2, -1.0, 1.0) * jnp.sin(angles)

    def rotary(u):
        return (u * cosines + pltpu.roll(u, LANES // 2, 1) * sines).astype(BF16)

    nt = (((1,), (1,)), ((), ()))
    loads["wk"].wait()
    loads["wv"].wait()
    kv_out[...] = jnp.zeros(kv_out.shape, BF16)
    wide = wk.shape[0]
    kv_out[0:2, 0:wide] = lax.dot_general(normed, wk[...], nt, preferred_element_type=F32).astype(BF16)
    kv_out[2:4, 0:wide] = lax.dot_general(normed, wv[...], nt, preferred_element_type=F32).astype(BF16)
    loads["wq"].wait()
    raw = jnp.dot(normed, wq[...], preferred_element_type=F32).astype(BF16).astype(F32)
    q_own = rotary(raw)
    q_in[me] = q_own
    kv_in[seat] = kv_out[...]

    pl.semaphore_wait(barrier, n - 1)

    def send_q(p, carry):
        pltpu.make_async_remote_copy(
            q_in.at[me], q_in.at[me], send_sem.at[0], recv_sem.at[0],
            device_id=to(lax.rem(me + p, n)), device_id_type=MESH,
        ).start()
        return carry

    lax.fori_loop(1, n, send_q, 0)

    def send_kv(p, carry):
        pltpu.make_async_remote_copy(
            kv_out, kv_in.at[seat], send_sem.at[1], recv_sem.at[1],
            device_id=to(plane * group + lax.rem(seat + p, group)), device_id_type=MESH,
        ).start()
        return carry

    lax.fori_loop(1, group, send_kv, 0)

    def wait_all(buf, count, k):
        views = buf.at[pl.ds(0, count)]
        both = pltpu.make_async_remote_copy(
            views, views, send_sem.at[k], recv_sem.at[k],
            device_id=to(lax.rem(me + 1, n)), device_id_type=MESH,
        )
        both.wait_recv()
        both.wait_send()

    loads["kc"].wait()
    loads["len"].wait()
    wait_all(q_in, n - 1, 0)

    live = jnp.clip(len_s[0] - me * (total // group), 0, total // group) * group
    lane_w = lax.broadcasted_iota(jnp.int32, (rows, width), 1)
    head_w = lane_w % group
    queries = q_in[...].reshape(n * steps, LANES)

    def score(c, top):
        keys = kc[pl.ds(pl.multiple_of(c * width, width), width), :]
        every = lax.dot_general(queries, keys, nt, preferred_element_type=F32)
        mine = every[0:rows]
        for g in range(1, n // group):
            mine = jnp.where(head_w == g, every[rows * g : rows * (g + 1)], mine)
        mine = jnp.where(lane_w + c * width < live, mine * scale, NEG)
        scores[c] = mine
        for t in range(width // LANES):
            top = jnp.maximum(top, mine[:, LANES * t : LANES * (t + 1)])
        return top

    top = lax.fori_loop(0, chunks, score, jnp.full((rows, LANES), NEG, F32), unroll=True)
    top = lane_class_reduce(top, jnp.maximum, group)

    loads["vc"].wait()
    lane_r = lax.broadcasted_iota(jnp.int32, (rows, LANES), 1)
    picks = [jnp.where(lane_r % group == g, 1.0, 0.0).astype(BF16) for g in range(n // group)]

    def weigh(c, carried):
        den, num = carried
        tiles = []
        for t in range(width // LANES):
            s = scores[c, :, LANES * t : LANES * (t + 1)]
            w = jnp.where(lane_r + (c * width + LANES * t) < live, jnp.exp(s - top), 0.0)
            den = den + w
            tiles.append(w.astype(BF16))
        spread = jnp.concatenate(
            [jnp.concatenate([w * pick for w in tiles], axis=1) for pick in picks], axis=0
        )
        values = vc[pl.ds(pl.multiple_of(c * width, width), width), :]
        return den, num + jnp.dot(spread, values, preferred_element_type=F32)

    den, num = lax.fori_loop(
        0, chunks, weigh,
        (jnp.zeros((rows, LANES), F32), jnp.zeros((n * steps, LANES), F32)), unroll=True
    )
    den = lane_class_reduce(den, jnp.add, group)

    def terms(v, count):
        out = []
        for _ in range(count):
            head = v.astype(BF16).astype(F32)
            out.append(head)
            v = v - head
        return out

    side = jnp.zeros((rows, LANES), F32)
    for k, term in enumerate(terms(top, 3) + terms(den, 3)):
        side = jnp.where(lane_r // group == k, term, side)
    side = side.astype(BF16)
    num = num.astype(BF16)
    for h in range(n):
        j = h % group
        part_out[h, 0:2, :] = num[2 * h : 2 * h + 2]
        part_out[h, 2:4, :] = side[2 * j : 2 * j + 2]
    part_in[me] = part_out[me]

    def send_part(p, carry):
        peer = lax.rem(me + p, n)
        pltpu.make_async_remote_copy(
            part_out.at[peer], part_in.at[me], send_sem.at[2], recv_sem.at[2],
            device_id=to(peer), device_id_type=MESH,
        ).start()
        return carry

    lax.fori_loop(1, n, send_part, 0)

    wait_all(kv_in, group - 1, 1)
    fresh = jnp.zeros((4, LANES), F32)
    for j in range(group):
        piece = kv_in[j].astype(F32)
        fresh = fresh + (pltpu.roll(piece, wide * j, 1) if j else piece)
    new_key = rotary(fresh[0:2]).astype(F32)
    new_val = fresh[2:4]
    qf = q_own.astype(F32)
    second = lax.broadcasted_iota(jnp.int32, (steps, 1), 0) > 0
    s0 = jnp.sum(qf * new_key[0:1], -1, keepdims=True) * scale
    s1 = jnp.sum(qf * new_key[1:2], -1, keepdims=True) * scale
    s1 = jnp.where(second, s1, NEG)

    wait_all(part_in, n - 1, 2)
    parts = part_in[...].astype(F32)
    lane_p = lax.broadcasted_iota(jnp.int32, (n, 2, LANES), 2)
    ours = lane_p % group == plane
    numer = parts[:, 0:2, :]
    extra = parts[:, 2:4, :]
    tops = jnp.sum(jnp.where(ours & (lane_p < 3 * group), extra, 0.0), -1, keepdims=True)
    dens = jnp.sum(
        jnp.where(ours & (lane_p >= 3 * group) & (lane_p < 6 * group), extra, 0.0), -1, keepdims=True
    )
    final = jnp.maximum(jnp.max(tops, 0), jnp.maximum(s0, s1))
    factor = jnp.exp(tops - final[None])
    w0 = jnp.exp(s0 - final)
    w1 = jnp.where(second, jnp.exp(s1 - final), 0.0)
    bottom = jnp.sum(factor * dens, 0) + w0 + w1
    upper = (
        jnp.sum(factor * numer, 0)
        + w0.astype(BF16).astype(F32) * new_val[0:1]
        + w1.astype(BF16).astype(F32) * new_val[1:2]
    )
    head_out = (upper / bottom).astype(BF16)

    loads["wo"].wait()
    span = group * LANES
    order = list(range(planes))
    for at in range(0, planes, 1):
        for target in order[at : at + 1]:
            cols = pl.ds(target * span, span)
            block = jnp.dot(head_out, wo[:, cols], preferred_element_type=F32).astype(BF16)
            for j in range(group):
                proj_out[target * group + j] = block[:, LANES * j : LANES * (j + 1)]
        for target in order[at : at + 1]:
            def send_proj(j, carry, target=target):
                peer = target * group + lax.rem(seat + j, group)

                @pl.when(peer != me)
                def _():
                    pltpu.make_async_remote_copy(
                        proj_out.at[peer], proj_in.at[me], send_sem.at[3], recv_sem.at[3],
                        device_id=to(peer), device_id_type=MESH,
                    ).start()

                return carry

            lax.fori_loop(0, group, send_proj, 0)
    proj_in[me] = proj_out[me]
    wait_all(proj_in, n - 1, 3)
    out_ref[...] = jnp.sum(proj_in[...].astype(F32), 0).astype(BF16)


def on_device(
    hidden, norm_gain, w_query, w_key, w_value, w_out, cache_keys, cache_values, lengths, positions
):
    n = lax.axis_size("ctx")
    steps, _, depth = hidden.shape
    _, span, group_count, head_size = cache_keys.shape
    group = n // group_count
    total = span * group_count
    chunks = 8
    half = head_size // 2
    inverse = theta_base ** (-(np.arange(half, dtype=np.float64) * 2.0 / head_size))
    inverse = np.tile(np.concatenate([inverse, inverse]).astype(np.float32)[None], (8, 1))
    dims = (n, group, steps, chunks, 1.0 / math.sqrt(head_size))
    anywhere = pl.BlockSpec(memory_space=pl.ANY)
    rows = 2 * group
    in_hbm = lambda a: pltpu.with_memory_space_constraint(a, pltpu.HBM)
    out = pl.pallas_call(
        functools.partial(kernel, dims),
        out_shape=jax.ShapeDtypeStruct((steps, w_out.shape[1] // n), BF16),
        in_specs=[anywhere] * 11,
        out_specs=pl.BlockSpec(memory_space=pltpu.VMEM),
        scratch_shapes=[
            pltpu.SMEM((1,), jnp.int32),
            pltpu.SMEM((1,), jnp.int32),
            pltpu.VMEM((steps, depth), BF16),
            pltpu.VMEM((depth // LANES, LANES), BF16),
            pltpu.VMEM((8, LANES), F32),
            pltpu.VMEM((depth, LANES), BF16),
            pltpu.VMEM((w_key.shape[1], depth), BF16),
            pltpu.VMEM((w_value.shape[1], depth), BF16),
            pltpu.VMEM(w_out.shape, BF16),
            pltpu.VMEM((total, head_size), BF16),
            pltpu.VMEM((total, head_size), BF16),
            pltpu.VMEM((n, steps, LANES), BF16),
            pltpu.VMEM((4, LANES), BF16),
            pltpu.VMEM((group, 4, LANES), BF16),
            pltpu.VMEM((chunks, rows, total // chunks), F32),
            pltpu.VMEM((n, 4, LANES), BF16),
            pltpu.VMEM((n, 4, LANES), BF16),
            pltpu.VMEM((n, steps, LANES), BF16),
            pltpu.VMEM((n, steps, LANES), BF16),
            pltpu.SemaphoreType.DMA((11,)),
            pltpu.SemaphoreType.DMA((4,)),
            pltpu.SemaphoreType.DMA((4,)),
        ],
        compiler_params=pltpu.CompilerParams(
            collective_id=0, has_side_effects=True, vmem_limit_bytes=48 * 1024 * 1024
        ),
        cost_estimate=pl.CostEstimate(flops=2**30, bytes_accessed=13 * 2**20, transcendentals=2**18),
        name="decode",
    )(
        positions,
        lengths,
        *map(in_hbm, (
            hidden.reshape(steps, depth),
            norm_gain.reshape(depth // LANES, LANES),
            jnp.asarray(inverse),
            w_query,
            w_key.T,
            w_value.T,
            w_out,
            cache_keys.reshape(total, head_size),
            cache_values.reshape(total, head_size),
        )),
    )
    return out[:, :, None]


def solution(mesh):
    in_specs = (
        P(None, "rows", None),
        P(),
        P(None, "ctx"),
        P(None, "ctx"),
        P(None, "ctx"),
        P("ctx", None),
        P("rows", "ctx", None, None),
        P("rows", "ctx", None, None),
        P("rows"),
        P("rows"),
    )
    out_specs = P(None, "ctx", "rows")
    return jax.shard_map(
        on_device, mesh=mesh, in_specs=in_specs, out_specs=out_specs, check_vma=False
    )
```

```python
import functools
import math

import jax
import jax.numpy as jnp
import numpy as np
from jax import lax
from jax.experimental import pallas as pl
from jax.experimental.pallas import tpu as pltpu
from jax.sharding import PartitionSpec as P

theta_base = 500000.0
epsilon = 1e-05
NEG = -1e30
LANES = 128
MESH = pl.DeviceIdType.MESH
F32 = jnp.float32
BF16 = jnp.bfloat16


def to(peer):
    return {"ctx": peer}


def lane_class_reduce(x, op, period):
    shift = period
    while shift < LANES:
        x = op(x, pltpu.roll(x, shift, 1))
        shift *= 2
    return x


def kernel(
    dims,
    pos_hbm, len_hbm, hid_hbm, gain_hbm, inv_hbm, wq_hbm, wk_hbm, wv_hbm, wo_hbm, kc_hbm, vc_hbm,
    out_ref,
    pos_s, len_s, hid, gain, inv, wq, wk, wv, wo, kc, vc,
    q_in, kv_out, kv_in, scores, part_out, part_in, proj_out, proj_in,
    load_sem, send_sem, recv_sem,
):
    n, group, steps, chunks, scale = dims
    me = lax.axis_index("ctx")
    plane = me // group
    seat = me - plane * group
    planes = n // group
    rows = 2 * group
    total = kc.shape[0]
    width = total // chunks

    loads = {}

    def load(**pairs):
        for name, (src, dst) in pairs.items():
            loads[name] = pltpu.make_async_copy(src, dst, load_sem.at[len(loads)])
            loads[name].start()

    load(hid=(hid_hbm, hid), gain=(gain_hbm, gain), wq=(wq_hbm, wq), wk=(wk_hbm, wk), wv=(wv_hbm, wv))
    barrier = pltpu.get_barrier_semaphore()

    def greet(p, carry):
        pl.semaphore_signal(barrier, inc=1, device_id=to(lax.rem(me + p, n)), device_id_type=MESH)
        return carry

    lax.fori_loop(1, n, greet, 0, unroll=9)

    load(pos=(pos_hbm, pos_s), inv=(inv_hbm, inv), len=(len_hbm, len_s))
    load(kc=(kc_hbm, kc), vc=(vc_hbm, vc), wo=(wo_hbm, wo))

    loads["hid"].wait()
    loads["gain"].wait()
    x = hid[...].astype(F32)
    x = x * lax.rsqrt(jnp.mean(x * x, -1, keepdims=True) + epsilon)
    normed = jnp.concatenate(
        [
            (x[:, LANES * r : LANES * (r + 1)] * gain[r : r + 1, :].astype(F32)).astype(BF16)
            for r in range(gain.shape[0])
        ],
        axis=1,
    )
    loads["pos"].wait()
    loads["inv"].wait()
    step_row = lax.broadcasted_iota(jnp.int32, (steps, LANES), 0)
    lane2 = lax.broadcasted_iota(jnp.int32, (steps, LANES), 1)
    angles = (pos_s[0] + step_row).astype(F32) * inv[0:1, :]
    cosines = jnp.cos(angles)
    sines = jnp.where(lane2 < LANES // 2, -1.0, 1.0) * jnp.sin(angles)

    def rotary(u):
        return (u * cosines + pltpu.roll(u, LANES // 2, 1) * sines).astype(BF16)

    nt = (((1,), (1,)), ((), ()))
    loads["wk"].wait()
    loads["wv"].wait()
    kv_out[...] = jnp.zeros(kv_out.shape, BF16)
    wide = wk.shape[0]
    kv_out[0:2, 0:wide] = lax.dot_general(normed, wk[...], nt, preferred_element_type=F32).astype(BF16)
    kv_out[2:4, 0:wide] = lax.dot_general(normed, wv[...], nt, preferred_element_type=F32).astype(BF16)
    loads["wq"].wait()
    raw = jnp.dot(normed, wq[...], preferred_element_type=F32).astype(BF16).astype(F32)
    q_own = rotary(raw)
    q_in[me] = q_own
    kv_in[seat] = kv_out[...]

    pl.semaphore_wait(barrier, n - 1)

    def send_q(p, carry):
        pltpu.make_async_remote_copy(
            q_in.at[me], q_in.at[me], send_sem.at[0], recv_sem.at[0],
            device_id=to(lax.rem(me + p, n)), device_id_type=MESH,
        ).start()
        return carry

    lax.fori_loop(1, n, send_q, 0, unroll=9)

    def send_kv(p, carry):
        pltpu.make_async_remote_copy(
            kv_out, kv_in.at[seat], send_sem.at[1], recv_sem.at[1],
            device_id=to(plane * group + lax.rem(seat + p, group)), device_id_type=MESH,
        ).start()
        return carry

    lax.fori_loop(1, group, send_kv, 0, unroll=True)

    def wait_all(buf, count, k):
        views = buf.at[pl.ds(0, count)]
        both = pltpu.make_async_remote_copy(
            views, views, send_sem.at[k], recv_sem.at[k],
            device_id=to(lax.rem(me + 1, n)), device_id_type=MESH,
        )
        both.wait_recv()
        both.wait_send()

    loads["kc"].wait()
    loads["len"].wait()
    wait_all(q_in, n - 1, 0)

    live = jnp.clip(len_s[0] - me * (total // group), 0, total // group) * group
    lane_w = lax.broadcasted_iota(jnp.int32, (rows, width), 1)
    head_w = lane_w % group
    queries = q_in[...].reshape(n * steps, LANES)

    def score(c, top):
        keys = kc[pl.ds(pl.multiple_of(c * width, width), width), :]
        every = lax.dot_general(queries, keys, nt, preferred_element_type=F32)
        mine = every[0:rows]
        for g in range(1, n // group):
            mine = jnp.where(head_w == g, every[rows * g : rows * (g + 1)], mine)
        mine = jnp.where(lane_w + c * width < live, mine * scale, NEG)
        scores[c] = mine
        for t in range(width // LANES):
            top = jnp.maximum(top, mine[:, LANES * t : LANES * (t + 1)])
        return top

    top = lax.fori_loop(0, chunks, score, jnp.full((rows, LANES), NEG, F32), unroll=True)
    top = lane_class_reduce(top, jnp.maximum, group)

    loads["vc"].wait()
    lane_r = lax.broadcasted_iota(jnp.int32, (rows, LANES), 1)
    picks = [jnp.where(lane_r % group == g, 1.0, 0.0).astype(BF16) for g in range(n // group)]

    def weigh(c, carried):
        den, num = carried
        tiles = []
        for t in range(width // LANES):
            s = scores[c, :, LANES * t : LANES * (t + 1)]
            w = jnp.where(lane_r + (c * width + LANES * t) < live, jnp.exp(s - top), 0.0)
            den = den + w
            tiles.append(w.astype(BF16))
        spread = jnp.concatenate(
            [jnp.concatenate([w * pick for w in tiles], axis=1) for pick in picks], axis=0
        )
        values = vc[pl.ds(pl.multiple_of(c * width, width), width), :]
        return den, num + jnp.dot(spread, values, preferred_element_type=F32)

    den, num = lax.fori_loop(
        0, chunks, weigh,
        (jnp.zeros((rows, LANES), F32), jnp.zeros((n * steps, LANES), F32)), unroll=True
    )
    den = lane_class_reduce(den, jnp.add, group)

    def terms(v, count):
        out = []
        for _ in range(count):
            head = v.astype(BF16).astype(F32)
            out.append(head)
            v = v - head
        return out

    side = jnp.zeros((rows, LANES), F32)
    for k, term in enumerate(terms(top, 3) + terms(den, 3)):
        side = jnp.where(lane_r // group == k, term, side)
    side = side.astype(BF16)
    num = num.astype(BF16)
    for h in range(n):
        j = h % group
        part_out[h, 0:2, :] = num[2 * h : 2 * h + 2]
        part_out[h, 2:4, :] = side[2 * j : 2 * j + 2]
    part_in[me] = part_out[me]

    def send_part(p, carry):
        peer = lax.rem(me + p, n)
        pltpu.make_async_remote_copy(
            part_out.at[peer], part_in.at[me], send_sem.at[2], recv_sem.at[2],
            device_id=to(peer), device_id_type=MESH,
        ).start()
        return carry

    lax.fori_loop(1, n, send_part, 0, unroll=9)

    wait_all(kv_in, group - 1, 1)
    fresh = jnp.zeros((4, LANES), F32)
    for j in range(group):
        piece = kv_in[j].astype(F32)
        fresh = fresh + (pltpu.roll(piece, wide * j, 1) if j else piece)
    new_key = rotary(fresh[0:2]).astype(F32)
    new_val = fresh[2:4]
    qf = q_own.astype(F32)
    second = lax.broadcasted_iota(jnp.int32, (steps, 1), 0) > 0
    s0 = jnp.sum(qf * new_key[0:1], -1, keepdims=True) * scale
    s1 = jnp.sum(qf * new_key[1:2], -1, keepdims=True) * scale
    s1 = jnp.where(second, s1, NEG)

    wait_all(part_in, n - 1, 2)
    parts = part_in[...].astype(F32)
    lane_p = lax.broadcasted_iota(jnp.int32, (n, 2, LANES), 2)
    ours = lane_p % group == plane
    numer = parts[:, 0:2, :]
    extra = parts[:, 2:4, :]
    tops = jnp.sum(jnp.where(ours & (lane_p < 3 * group), extra, 0.0), -1, keepdims=True)
    dens = jnp.sum(
        jnp.where(ours & (lane_p >= 3 * group) & (lane_p < 6 * group), extra, 0.0), -1, keepdims=True
    )
    final = jnp.maximum(jnp.max(tops, 0), jnp.maximum(s0, s1))
    factor = jnp.exp(tops - final[None])
    w0 = jnp.exp(s0 - final)
    w1 = jnp.where(second, jnp.exp(s1 - final), 0.0)
    bottom = jnp.sum(factor * dens, 0) + w0 + w1
    upper = (
        jnp.sum(factor * numer, 0)
        + w0.astype(BF16).astype(F32) * new_val[0:1]
        + w1.astype(BF16).astype(F32) * new_val[1:2]
    )
    head_out = (upper / bottom).astype(BF16)

    loads["wo"].wait()
    span = group * LANES
    order = list(range(planes))

    def send_proj(peer):
        pltpu.make_async_remote_copy(
            proj_out.at[peer], proj_in.at[me], send_sem.at[3], recv_sem.at[3],
            device_id=to(peer), device_id_type=MESH,
        ).start()

    for at in range(0, planes, 1):
        for target in order[at : at + 1]:
            cols = pl.ds(target * span, span)
            block = jnp.dot(head_out, wo[:, cols], preferred_element_type=F32).astype(BF16)
            for j in range(group):
                proj_out[target * group + j] = block[:, LANES * j : LANES * (j + 1)]
        for target in order[at : at + 1]:
            for j in range(1, group):
                send_proj(target * group + lax.rem(seat + j, group))
    for target in order:
        @pl.when(target != plane)
        def _(target=target):
            send_proj(target * group + seat)

    proj_in[me] = proj_out[me]
    wait_all(proj_in, n - 1, 3)
    out_ref[...] = jnp.sum(proj_in[...].astype(F32), 0).astype(BF16)


def on_device(
    hidden, norm_gain, w_query, w_key, w_value, w_out, cache_keys, cache_values, lengths, positions
):
    n = lax.axis_size("ctx")
    steps, _, depth = hidden.shape
    _, span, group_count, head_size = cache_keys.shape
    group = n // group_count
    total = span * group_count
    chunks = 8
    half = head_size // 2
    inverse = theta_base ** (-(np.arange(half, dtype=np.float64) * 2.0 / head_size))
    inverse = np.tile(np.concatenate([inverse, inverse]).astype(np.float32)[None], (8, 1))
    dims = (n, group, steps, chunks, 1.0 / math.sqrt(head_size))
    anywhere = pl.BlockSpec(memory_space=pl.ANY)
    rows = 2 * group
    in_hbm = lambda a: pltpu.with_memory_space_constraint(a, pltpu.HBM)
    out = pl.pallas_call(
        functools.partial(kernel, dims),
        out_shape=jax.ShapeDtypeStruct((steps, w_out.shape[1] // n), BF16),
        in_specs=[anywhere] * 11,
        out_specs=pl.BlockSpec(memory_space=pltpu.VMEM),
        scratch_shapes=[
            pltpu.SMEM((1,), jnp.int32),
            pltpu.SMEM((1,), jnp.int32),
            pltpu.VMEM((steps, depth), BF16),
            pltpu.VMEM((depth // LANES, LANES), BF16),
            pltpu.VMEM((8, LANES), F32),
            pltpu.VMEM((depth, LANES), BF16),
            pltpu.VMEM((w_key.shape[1], depth), BF16),
            pltpu.VMEM((w_value.shape[1], depth), BF16),
            pltpu.VMEM(w_out.shape, BF16),
            pltpu.VMEM((total, head_size), BF16),
            pltpu.VMEM((total, head_size), BF16),
            pltpu.VMEM((n, steps, LANES), BF16),
            pltpu.VMEM((4, LANES), BF16),
            pltpu.VMEM((group, 4, LANES), BF16),
            pltpu.VMEM((chunks, rows, total // chunks), F32),
            pltpu.VMEM((n, 4, LANES), BF16),
            pltpu.VMEM((n, 4, LANES), BF16),
            pltpu.VMEM((n, steps, LANES), BF16),
            pltpu.VMEM((n, steps, LANES), BF16),
            pltpu.SemaphoreType.DMA((11,)),
            pltpu.SemaphoreType.DMA((4,)),
            pltpu.SemaphoreType.DMA((4,)),
        ],
        compiler_params=pltpu.CompilerParams(
            collective_id=0, has_side_effects=True, vmem_limit_bytes=48 * 1024 * 1024
        ),
        cost_estimate=pl.CostEstimate(flops=2**30, bytes_accessed=13 * 2**20, transcendentals=2**18),
        name="decode",
    )(
        positions,
        lengths,
        *map(in_hbm, (
            hidden.reshape(steps, depth),
            norm_gain.reshape(depth // LANES, LANES),
            jnp.asarray(inverse),
            w_query,
            w_key.T,
            w_value.T,
            w_out,
            cache_keys.reshape(total, head_size),
            cache_values.reshape(total, head_size),
        )),
    )
    return out[:, :, None]


def solution(mesh):
    in_specs = (
        P(None, "rows", None),
        P(),
        P(None, "ctx"),
        P(None, "ctx"),
        P(None, "ctx"),
        P("ctx", None),
        P("rows", "ctx", None, None),
        P("rows", "ctx", None, None),
        P("rows"),
        P("rows"),
    )
    out_specs = P(None, "ctx", "rows")
    return jax.shard_map(
        on_device, mesh=mesh, in_specs=in_specs, out_specs=out_specs, check_vma=False
    )
```

```python
import functools
import math

import jax
import jax.numpy as jnp
import numpy as np
from jax import lax
from jax.experimental import pallas as pl
from jax.experimental.pallas import tpu as pltpu
from jax.sharding import PartitionSpec as P

theta_base = 500000.0
epsilon = 1e-05
NEG = -1e30
LANES = 128
MESH = pl.DeviceIdType.MESH
F32 = jnp.float32
BF16 = jnp.bfloat16


def to(peer):
    return {"ctx": peer}


def lane_class_reduce(x, op, period):
    shift = period
    while shift < LANES:
        x = op(x, pltpu.roll(x, shift, 1))
        shift *= 2
    return x


def kernel(
    dims,
    pos_hbm, len_hbm, hid_hbm, gain_hbm, inv_hbm, wq_hbm, wk_hbm, wv_hbm, wo_hbm, kc_hbm, vc_hbm,
    out_ref,
    pos_s, len_s, hid, gain, inv, wq, wk, wv, wo, kc, vc,
    q_in, kv_out, kv_in, scores, part_out, part_in, proj_out, proj_in,
    load_sem, send_sem, recv_sem, q_sem, ready,
):
    n, group, steps, chunks, scale = dims
    me = lax.axis_index("ctx")
    plane = me // group
    seat = me - plane * group
    planes = n // group
    half = n // 2
    upper = plane >= planes // 2
    lower = plane < planes // 2
    rows = 2 * group
    total = kc.shape[0]
    width = total // chunks

    loads = {}

    def load(**pairs):
        for name, (src, dst) in pairs.items():
            loads[name] = pltpu.make_async_copy(src, dst, load_sem.at[len(loads)])
            loads[name].start()

    load(hid=(hid_hbm, hid), gain=(gain_hbm, gain), wq=(wq_hbm, wq), wk=(wk_hbm, wk), wv=(wv_hbm, wv))
    barrier = pltpu.get_barrier_semaphore()

    def others(start, act):
        def one(p, carry):
            act(lax.rem(me + p, half) + start)
            return carry

        lax.fori_loop(1, half, one, 0, unroll=half - 1)

    def across(start, act):
        def one(p, carry):
            act(lax.rem(me + p, half) + start)
            return carry

        lax.fori_loop(0, half, one, 0, unroll=half)

    def greet(peer):
        pl.semaphore_signal(barrier, inc=1, device_id=to(peer), device_id_type=MESH)

    @pl.when(lower)
    def _():
        others(0, greet)
        across(half, greet)

    @pl.when(upper)
    def _():
        others(half, greet)

    load(pos=(pos_hbm, pos_s), inv=(inv_hbm, inv), len=(len_hbm, len_s))
    load(kc=(kc_hbm, kc), vc=(vc_hbm, vc), wo=(wo_hbm, wo))

    loads["hid"].wait()
    loads["gain"].wait()
    x = hid[...].astype(F32)
    x = x * lax.rsqrt(jnp.mean(x * x, -1, keepdims=True) + epsilon)
    normed = jnp.concatenate(
        [
            (x[:, LANES * r : LANES * (r + 1)] * gain[r : r + 1, :].astype(F32)).astype(BF16)
            for r in range(gain.shape[0])
        ],
        axis=1,
    )
    loads["pos"].wait()
    loads["inv"].wait()
    step_row = lax.broadcasted_iota(jnp.int32, (steps, LANES), 0)
    lane2 = lax.broadcasted_iota(jnp.int32, (steps, LANES), 1)
    angles = (pos_s[0] + step_row).astype(F32) * inv[0:1, :]
    cosines = jnp.cos(angles)
    sines = jnp.where(lane2 < LANES // 2, -1.0, 1.0) * jnp.sin(angles)

    def rotary(u):
        return (u * cosines + pltpu.roll(u, LANES // 2, 1) * sines).astype(BF16)

    nt = (((1,), (1,)), ((), ()))
    loads["wk"].wait()
    loads["wv"].wait()
    kv_out[...] = jnp.zeros(kv_out.shape, BF16)
    wide = wk.shape[0]
    kv_out[0:2, 0:wide] = lax.dot_general(normed, wk[...], nt, preferred_element_type=F32).astype(BF16)
    kv_out[2:4, 0:wide] = lax.dot_general(normed, wv[...], nt, preferred_element_type=F32).astype(BF16)
    loads["wq"].wait()
    raw = jnp.dot(normed, wq[...], preferred_element_type=F32).astype(BF16).astype(F32)
    q_own = rotary(raw)
    q_in[me] = q_own
    kv_in[seat] = kv_out[...]

    def send_q(k):
        def one(peer):
            pltpu.make_async_remote_copy(
                q_in.at[me], q_in.at[me], send_sem.at[0], q_sem.at[k],
                device_id=to(peer), device_id_type=MESH,
            ).start()

        return one

    def queries_come(k, count):
        come = q_in.at[pl.ds(0, count)]
        pltpu.make_async_remote_copy(
            come, come, send_sem.at[0], q_sem.at[k],
            device_id=to(lax.rem(me + 1, n)), device_id_type=MESH,
        ).wait_recv()

    def queries_left(count):
        come = q_in.at[pl.ds(0, count)]
        pltpu.make_async_remote_copy(
            come, come, send_sem.at[0], q_sem.at[0],
            device_id=to(lax.rem(me + 1, n)), device_id_type=MESH,
        ).wait_send()

    quarter = planes // 4
    far = planes - quarter
    first_relay, last_relay = planes // 2 - 1, 0

    def relay(peer, slot):
        pl.semaphore_wait(ready.at[slot], 1)
        pltpu.make_async_remote_copy(
            q_in.at[pl.ds(0, half)], q_in.at[pl.ds(0, half)], send_sem.at[4 + slot], q_sem.at[0],
            device_id=to(peer), device_id_type=MESH,
        ).start()

    @pl.when(lower)
    def _():
        pl.semaphore_wait(barrier, half - 1)
        others(0, send_q(0))
        queries_come(0, half - 1)

    for where, start in ((first_relay, planes // 2), (last_relay, far)):
        @pl.when(plane == where)
        def _(start=start):
            for slot in range(quarter):
                relay((start + slot) * group + seat, slot)

    @pl.when(upper)
    def _():
        pl.semaphore_wait(barrier, n - 1)

    for start, where in ((planes // 2, first_relay), (far, last_relay)):
        for slot in range(quarter):
            @pl.when(plane == start + slot)
            def _(slot=slot, where=where):
                pl.semaphore_signal(
                    ready.at[slot], inc=1, device_id=to(where * group + seat), device_id_type=MESH
                )

    @pl.when(upper)
    def _():
        others(half, send_q(1))
        across(0, send_q(1))

    def send_kv(p, carry):
        pltpu.make_async_remote_copy(
            kv_out, kv_in.at[seat], send_sem.at[1], recv_sem.at[1],
            device_id=to(plane * group + lax.rem(seat + p, group)), device_id_type=MESH,
        ).start()
        return carry

    lax.fori_loop(1, group, send_kv, 0, unroll=True)

    def wait_all(buf, count, k):
        views = buf.at[pl.ds(0, count)]
        both = pltpu.make_async_remote_copy(
            views, views, send_sem.at[k], recv_sem.at[k],
            device_id=to(lax.rem(me + 1, n)), device_id_type=MESH,
        )
        both.wait_recv()
        both.wait_send()

    loads["kc"].wait()
    loads["len"].wait()

    @pl.when(lower)
    def _():
        queries_come(1, half)
        queries_left(half - 1)

    for where in (first_relay, last_relay):
        @pl.when(plane == where)
        def _():
            for slot in range(quarter):
                block = q_in.at[pl.ds(0, half)]
                pltpu.make_async_remote_copy(
                    block, block, send_sem.at[4 + slot], q_sem.at[0],
                    device_id=to(lax.rem(me + 1, n)), device_id_type=MESH,
                ).wait_send()

    @pl.when(upper)
    def _():
        queries_come(1, half - 1)
        queries_come(0, half)
        queries_left(n - 1)


    live = jnp.clip(len_s[0] - me * (total // group), 0, total // group) * group
    lane_w = lax.broadcasted_iota(jnp.int32, (rows, width), 1)
    head_w = lane_w % group
    queries = q_in[...].reshape(n * steps, LANES)

    def score(c, top):
        keys = kc[pl.ds(pl.multiple_of(c * width, width), width), :]
        every = lax.dot_general(queries, keys, nt, preferred_element_type=F32)
        mine = every[0:rows]
        for g in range(1, n // group):
            mine = jnp.where(head_w == g, every[rows * g : rows * (g + 1)], mine)
        mine = jnp.where(lane_w + c * width < live, mine * scale, NEG)
        scores[c] = mine
        for t in range(width // LANES):
            top = jnp.maximum(top, mine[:, LANES * t : LANES * (t + 1)])
        return top

    top = lax.fori_loop(0, chunks, score, jnp.full((rows, LANES), NEG, F32), unroll=True)
    top = lane_class_reduce(top, jnp.maximum, group)

    loads["vc"].wait()
    lane_r = lax.broadcasted_iota(jnp.int32, (rows, LANES), 1)
    picks = [jnp.where(lane_r % group == g, 1.0, 0.0).astype(BF16) for g in range(n // group)]

    def weigh(c, carried):
        den, num = carried
        tiles = []
        for t in range(width // LANES):
            s = scores[c, :, LANES * t : LANES * (t + 1)]
            w = jnp.where(lane_r + (c * width + LANES * t) < live, jnp.exp(s - top), 0.0)
            den = den + w
            tiles.append(w.astype(BF16))
        spread = jnp.concatenate(
            [jnp.concatenate([w * pick for w in tiles], axis=1) for pick in picks], axis=0
        )
        values = vc[pl.ds(pl.multiple_of(c * width, width), width), :]
        return den, num + jnp.dot(spread, values, preferred_element_type=F32)

    den, num = lax.fori_loop(
        0, chunks, weigh,
        (jnp.zeros((rows, LANES), F32), jnp.zeros((n * steps, LANES), F32)), unroll=True
    )
    den = lane_class_reduce(den, jnp.add, group)

    def terms(v, count):
        out = []
        for _ in range(count):
            head = v.astype(BF16).astype(F32)
            out.append(head)
            v = v - head
        return out

    side = jnp.zeros((rows, LANES), F32)
    for k, term in enumerate(terms(top, 3) + terms(den, 3)):
        side = jnp.where(lane_r // group == k, term, side)
    side = side.astype(BF16)
    num = num.astype(BF16)
    for h in range(n):
        j = h % group
        part_out[h, 0:2, :] = num[2 * h : 2 * h + 2]
        part_out[h, 2:4, :] = side[2 * j : 2 * j + 2]
    part_in[me] = part_out[me]

    def send_part(p, carry):
        peer = lax.rem(me + p, n)
        pltpu.make_async_remote_copy(
            part_out.at[peer], part_in.at[me], send_sem.at[2], recv_sem.at[2],
            device_id=to(peer), device_id_type=MESH,
        ).start()
        return carry

    lax.fori_loop(1, n, send_part, 0, unroll=9)

    wait_all(kv_in, group - 1, 1)
    fresh = jnp.zeros((4, LANES), F32)
    for j in range(group):
        piece = kv_in[j].astype(F32)
        fresh = fresh + (pltpu.roll(piece, wide * j, 1) if j else piece)
    new_key = rotary(fresh[0:2]).astype(F32)
    new_val = fresh[2:4]
    qf = q_own.astype(F32)
    second = lax.broadcasted_iota(jnp.int32, (steps, 1), 0) > 0
    s0 = jnp.sum(qf * new_key[0:1], -1, keepdims=True) * scale
    s1 = jnp.sum(qf * new_key[1:2], -1, keepdims=True) * scale
    s1 = jnp.where(second, s1, NEG)

    wait_all(part_in, n - 1, 2)
    parts = part_in[...].astype(F32)
    lane_p = lax.broadcasted_iota(jnp.int32, (n, 2, LANES), 2)
    ours = lane_p % group == plane
    numer = parts[:, 0:2, :]
    extra = parts[:, 2:4, :]
    tops = jnp.sum(jnp.where(ours & (lane_p < 3 * group), extra, 0.0), -1, keepdims=True)
    dens = jnp.sum(
        jnp.where(ours & (lane_p >= 3 * group) & (lane_p < 6 * group), extra, 0.0), -1, keepdims=True
    )
    final = jnp.maximum(jnp.max(tops, 0), jnp.maximum(s0, s1))
    factor = jnp.exp(tops - final[None])
    w0 = jnp.exp(s0 - final)
    w1 = jnp.where(second, jnp.exp(s1 - final), 0.0)
    bottom = jnp.sum(factor * dens, 0) + w0 + w1
    upper = (
        jnp.sum(factor * numer, 0)
        + w0.astype(BF16).astype(F32) * new_val[0:1]
        + w1.astype(BF16).astype(F32) * new_val[1:2]
    )
    head_out = (upper / bottom).astype(BF16)

    loads["wo"].wait()
    span = group * LANES
    order = list(range(planes))

    def send_proj(peer):
        pltpu.make_async_remote_copy(
            proj_out.at[peer], proj_in.at[me], send_sem.at[3], recv_sem.at[3],
            device_id=to(peer), device_id_type=MESH,
        ).start()

    for at in range(0, planes, 1):
        for target in order[at : at + 1]:
            cols = pl.ds(target * span, span)
            block = jnp.dot(head_out, wo[:, cols], preferred_element_type=F32).astype(BF16)
            for j in range(group):
                proj_out[target * group + j] = block[:, LANES * j : LANES * (j + 1)]
        for target in order[at : at + 1]:
            for j in range(1, group):
                send_proj(target * group + lax.rem(seat + j, group))
    for target in order:
        @pl.when(target != plane)
        def _(target=target):
            send_proj(target * group + seat)

    proj_in[me] = proj_out[me]
    wait_all(proj_in, n - 1, 3)
    out_ref[...] = jnp.sum(proj_in[...].astype(F32), 0).astype(BF16)


def on_device(
    hidden, norm_gain, w_query, w_key, w_value, w_out, cache_keys, cache_values, lengths, positions
):
    n = lax.axis_size("ctx")
    steps, _, depth = hidden.shape
    _, span, group_count, head_size = cache_keys.shape
    group = n // group_count
    total = span * group_count
    chunks = 16
    half = head_size // 2
    inverse = theta_base ** (-(np.arange(half, dtype=np.float64) * 2.0 / head_size))
    inverse = np.tile(np.concatenate([inverse, inverse]).astype(np.float32)[None], (8, 1))
    dims = (n, group, steps, chunks, 1.0 / math.sqrt(head_size))
    anywhere = pl.BlockSpec(memory_space=pl.ANY)
    rows = 2 * group
    in_hbm = lambda a: pltpu.with_memory_space_constraint(a, pltpu.HBM)
    out = pl.pallas_call(
        functools.partial(kernel, dims),
        out_shape=jax.ShapeDtypeStruct((steps, w_out.shape[1] // n), BF16),
        in_specs=[anywhere] * 11,
        out_specs=pl.BlockSpec(memory_space=pltpu.VMEM),
        scratch_shapes=[
            pltpu.SMEM((1,), jnp.int32),
            pltpu.SMEM((1,), jnp.int32),
            pltpu.VMEM((steps, depth), BF16),
            pltpu.VMEM((depth // LANES, LANES), BF16),
            pltpu.VMEM((8, LANES), F32),
            pltpu.VMEM((depth, LANES), BF16),
            pltpu.VMEM((w_key.shape[1], depth), BF16),
            pltpu.VMEM((w_value.shape[1], depth), BF16),
            pltpu.VMEM(w_out.shape, BF16),
            pltpu.VMEM((total, head_size), BF16),
            pltpu.VMEM((total, head_size), BF16),
            pltpu.VMEM((n, steps, LANES), BF16),
            pltpu.VMEM((4, LANES), BF16),
            pltpu.VMEM((group, 4, LANES), BF16),
            pltpu.VMEM((chunks, rows, total // chunks), F32),
            pltpu.VMEM((n, 4, LANES), BF16),
            pltpu.VMEM((n, 4, LANES), BF16),
            pltpu.VMEM((n, steps, LANES), BF16),
            pltpu.VMEM((n, steps, LANES), BF16),
            pltpu.SemaphoreType.DMA((11,)),
            pltpu.SemaphoreType.DMA((4 + group_count // 4,)),
            pltpu.SemaphoreType.DMA((4,)),
            pltpu.SemaphoreType.DMA((2,)),
            pltpu.SemaphoreType.REGULAR((group_count // 4,)),
        ],
        compiler_params=pltpu.CompilerParams(
            collective_id=0, has_side_effects=True, vmem_limit_bytes=48 * 1024 * 1024
        ),
        cost_estimate=pl.CostEstimate(flops=2**30, bytes_accessed=13 * 2**20, transcendentals=2**18),
        name="decode",
    )(
        positions,
        lengths,
        *map(in_hbm, (
            hidden.reshape(steps, depth),
            norm_gain.reshape(depth // LANES, LANES),
            jnp.asarray(inverse),
            w_query,
            w_key.T,
            w_value.T,
            w_out,
            cache_keys.reshape(total, head_size),
            cache_values.reshape(total, head_size),
        )),
    )
    return out[:, :, None]


def solution(mesh):
    in_specs = (
        P(None, "rows", None),
        P(),
        P(None, "ctx"),
        P(None, "ctx"),
        P(None, "ctx"),
        P("ctx", None),
        P("rows", "ctx", None, None),
        P("rows", "ctx", None, None),
        P("rows"),
        P("rows"),
    )
    out_specs = P(None, "ctx", "rows")
    return jax.shard_map(
        on_device, mesh=mesh, in_specs=in_specs, out_specs=out_specs, check_vma=False
    )
```
